32 devices in a mesh: seq: 16 (over z, y, core), mp: 2 (over x).
Axes of the slice: x: 2, y: 2, z: 4, core: 2. Of those that a mesh axis runs over, the one named last changes fastest.
Arguments:
- hidden: bfloat16 [4096, 2048], P('seq'), may hold values from -6 to 6
- ids: int32 [4096], P('seq'), may hold values from 0 to 4, as said below
- w_value: bfloat16 [2048, 2048], P(None, 'mp'), may hold values from -0.125 to 0.125
- w_bc: bfloat16 [2048, 2, 64], P(None, 'mp'), may hold values from -0.015625 to 0.015625
- w_step: bfloat16 [2048, 16], P(None, 'mp'), may hold values from -0.125 to 0.125
- step_bias: float32 [16], P('mp'), may hold values from -1 to 1
- decay_log: float32 [16], P('mp'), may hold values from -12 to -2
- skip: float32 [16], P('mp'), may hold values from 0.5 to 1.5
- norm_gain: float32 [2048], P('mp'), may hold values from 0.1 to 1.9
- w_out: bfloat16 [2048, 2048], P('mp'), may hold values from -0.125 to 0.125
- cotangent: bfloat16 [4096, 2048], P('seq'), may hold values from -6 to 6
Outputs:
- out: bfloat16 [4096, 2048], P('seq', 'mp')
- d_hidden: bfloat16 [4096, 2048], P('seq', 'mp')
The draws below stay inside these ranges and needn't reach their ends.
Inputs may be any that keep to these rules, and one draw needn't show every extreme that they name: `ids`: 4 marks an unknown base (N); such bases come in runs.
All inputs are finite; a program needn't handle non-finite values.
Results may differ from the reference program's by a relative error of at most 0.014.
Values may be sent and summed in bfloat16 or wider, within the bound.
A program may use at most 320 MiB of HBM per device.

```python
from functools import partial
import jax
import jax.numpy as jnp
from jax import lax

D = 2048
HEADS = 16
HEAD_DIM = 128
STATE = 32
GROUPS = 2
RUNS = 4
L_DEV = 256
INNER = 2048
TOTAL = 4096


def draw_ids(key, part):
    key_bases, key_starts, key_lengths = jax.random.split(key, 3)
    bases = jax.random.randint(key_bases, (TOTAL,), 0, 4)
    starts = jax.random.randint(key_starts, (RUNS,), 0, TOTAL)
    lengths = jax.random.randint(key_lengths, (RUNS,), 1, 2 * L_DEV)
    position = jnp.arange(TOTAL)
    inside = (position[None, :] >= starts[:, None]) & (position[None, :] < starts[:, None] + lengths[:, None])
    return jnp.where(jnp.any(inside, axis=0), 4, bases).astype(jnp.int32)


def draw_decay_log(key, part):
    key_kind, key_slow, key_fast = jax.random.split(key, 3)
    slow_heads = jax.random.uniform(key_kind, (HEADS,)) < 0.5
    slow_rate = jax.random.uniform(key_slow, (HEADS,), minval=0.3, maxval=1.5) / TOTAL
    fast_rate = jax.random.uniform(key_fast, (HEADS,), minval=0.02, maxval=0.05)
    return jnp.log(jnp.where(slow_heads, slow_rate, fast_rate)).astype(jnp.float32)


def levels(key, extent, cuts, low, top_value):
    gain, own = 1.0, jax.random.fold_in(key, 6)
    for axis_at, blocks in cuts:
        draws = jnp.exp(jax.random.uniform(jax.random.fold_in(own, axis_at), (blocks,), jnp.float32, low / len(cuts), top_value / len(cuts)))
        gain = gain * jnp.repeat(draws, extent[axis_at] // blocks).reshape([-1 if axis == axis_at else 1 for axis in range(len(extent))])
    return gain


def bell_draw(own_key, shape, scale, limit, shards=(), held_as=jnp.bfloat16):
    values = scale * jax.random.normal(own_key, shape, jnp.float32)
    if shards:
        values = values * levels(own_key, shape, shards, -0.22, 0.18)
    return jnp.clip(values, -limit, limit).astype(held_as)


def setup_inputs(seed: int = 0) -> dict:
    key_of = jax.random.split(jax.random.key(seed), 12)
    hidden = bell_draw(key_of[0], (TOTAL, D), 1.0, 6.0, ((0, 16),))
    ids = draw_ids(jax.random.fold_in(key_of[11], 71), 0)
    w_value = bell_draw(key_of[2], (D, INNER), D ** -0.5, 0.125, ((1, 2),))
    w_bc = bell_draw(key_of[3], (D, GROUPS, 2 * STATE), (D * 64) ** -0.5, 0.015625, ((1, 2),))
    w_step = bell_draw(key_of[4], (D, HEADS), D ** -0.5, 0.125, ((1, 2),))
    step_bias = jnp.clip(jax.random.uniform(key_of[5], (HEADS,), jnp.float32, -1.0, 1.0) * levels(key_of[5], (HEADS,), ((0, 2),), -0.4, 0.0), -1.0, 1.0)
    decay_log = draw_decay_log(jax.random.fold_in(key_of[11], 71), 0)
    skip = jnp.clip(0.5 + 1.0 * jax.random.uniform(key_of[7], (HEADS,), jnp.float32) ** levels(key_of[7], (HEADS,), ((0, 2),), -0.2, 0.2), 0.5, 1.5)
    norm_gain = jnp.clip(1.0 + 0.18 * jax.random.normal(key_of[8], (INNER,), jnp.float32), 0.1, 1.9)
    w_out = bell_draw(key_of[9], (INNER, D), INNER ** -0.5, 0.125, ((0, 2),))
    cotangent = bell_draw(key_of[10], (TOTAL, D), 1.0, 6.0, ((0, 16),))
    return dict(hidden=hidden, ids=ids, w_value=w_value, w_bc=w_bc, w_step=w_step, step_bias=step_bias, decay_log=decay_log, skip=skip, norm_gain=norm_gain, w_out=w_out, cotangent=cotangent)


precise = lax.Precision.HIGHEST
epsilon = 1e-05

def block_pieces(values, b_matrix, c_matrix, step_size, log_decay, skip_vec):
    length, head_count, _ = values.shape
    groups = b_matrix.shape[1]
    per_group = head_count // groups
    cumulative = jnp.cumsum(log_decay, axis=0)
    cum_heads = cumulative.T
    spread_log = cum_heads[:, :, None] - cum_heads[:, None, :]
    row_index = lax.broadcasted_iota(jnp.int32, (length, length), 0)
    col_index = lax.broadcasted_iota(jnp.int32, (length, length), 1)
    decay_matrix = jnp.exp(jnp.where((row_index >= col_index)[None], spread_log, -1e+30))
    scores = jnp.einsum('tgn,sgn->gts', c_matrix, b_matrix, precision=precise)
    weights = (decay_matrix.reshape(groups, per_group, length, length) * scores[:, None]).reshape(head_count, length, length)
    scaled = values * step_size[:, :, None]
    local_out = jnp.einsum('hts,shp->thp', weights, scaled, precision=precise) + skip_vec[None, :, None] * values
    tail_decay = jnp.exp(cumulative[-1][None, :] - cumulative)
    b_heads = jnp.repeat(b_matrix, per_group, axis=1)
    end_state = jnp.einsum('sh,shp,shn->hpn', tail_decay, scaled, b_heads, precision=precise)
    return (local_out, cumulative, jnp.exp(cumulative[-1]), end_state)

def carry_term(c_matrix, cumulative, start_state):
    per_group = start_state.shape[0] // c_matrix.shape[1]
    c_heads = jnp.repeat(c_matrix, per_group, axis=1)
    return jnp.einsum('thn,hpn->thp', c_heads, start_state, precision=precise) * jnp.exp(cumulative)[:, :, None]

def group_norm(mixed_out, gain_vec, groups):
    length = mixed_out.shape[0]
    grouped = mixed_out.reshape(length, groups, -1)
    scale = lax.rsqrt(lax.optimization_barrier(jnp.mean(grouped * grouped, axis=2, keepdims=True)) + epsilon)
    return (grouped * scale).reshape(length, -1) * gain_vec[None, :]

def project(source, w_value, w_bc, w_step, head_count):
    length = source.shape[0]
    values = jnp.dot(source, w_value, preferred_element_type=jnp.float32).astype(jnp.bfloat16)
    groups = w_bc.shape[1]
    state_width = w_bc.shape[2] // 2
    mixed = jnp.dot(source, w_bc.reshape(w_bc.shape[0], -1), preferred_element_type=jnp.float32).astype(jnp.bfloat16)
    mixed = mixed.reshape(length, groups, 2 * state_width).astype(jnp.float32)
    step_raw = jnp.dot(source, w_step, preferred_element_type=jnp.float32)
    return (values.astype(jnp.float32).reshape(length, head_count, -1), mixed[:, :, :state_width], mixed[:, :, state_width:], step_raw)

def direction_run(inputs, consts, flipped):
    values, b_matrix, c_matrix, step_raw = inputs
    step_bias, decay_log, skip_vec, gain_vec = consts
    if flipped:
        values, b_matrix, c_matrix, step_raw = (values[::-1], b_matrix[::-1], c_matrix[::-1], step_raw[::-1])
    step_size = jax.nn.softplus(step_raw + step_bias[None, :])
    log_decay = -jnp.exp(decay_log)[None, :] * step_size
    count = values.shape[0] // L_DEV
    head_count = values.shape[1]

    def advance(state, block):
        vals, b_blk, c_blk, s_blk, l_blk = block
        local_out, cumulative, total_decay, end_state = block_pieces(vals, b_blk, c_blk, s_blk, l_blk, skip_vec)
        mixed_out = local_out + carry_term(c_blk, cumulative, state)
        return (total_decay[:, None, None] * state + end_state, group_norm(mixed_out, gain_vec, GROUPS))
    blocks = tuple((array.reshape((count, L_DEV) + array.shape[1:]) for array in (values, b_matrix, c_matrix, step_size, log_decay)))
    initial = jnp.zeros((head_count, HEAD_DIM, STATE), jnp.float32)
    _, normed = lax.scan(jax.checkpoint(advance), initial, blocks)
    normed = normed.reshape(values.shape[0], -1)
    if flipped:
        normed = normed[::-1]
    return normed

def times_transposed(left, right):
    return lax.dot_general(left, right, (((1,), (1,)), ((), ())), preferred_element_type=jnp.float32)

def input_terms(packed, w_value, w_bc, w_step):
    inner_width = w_value.shape[1]
    bc_width = w_bc.shape[1] * w_bc.shape[2]
    total_terms = times_transposed(packed[:, :inner_width], w_value)
    total_terms = total_terms + times_transposed(packed[:, inner_width:inner_width + bc_width], w_bc.reshape(w_bc.shape[0], -1))
    return total_terms + times_transposed(packed[:, inner_width + bc_width:], w_step)

def pack_grads(first, second):
    length = first[0].shape[0]
    d_values = (first[0] + second[0]).reshape(length, -1)
    d_bc = jnp.concatenate([first[1] + second[1], first[2] + second[2]], axis=2).reshape(length, -1)
    d_step = first[3] + second[3]
    return jnp.concatenate([d_values, d_bc, d_step], axis=1).astype(jnp.bfloat16)

def reference(hidden, ids, w_value, w_bc, w_step, step_bias, decay_log, skip, norm_gain, w_out, cotangent):
    consts = (step_bias, decay_log, skip, norm_gain)
    normed = []
    local_back = []
    for source in (hidden, hidden[:, ::-1]):
        inputs = project(source, w_value, w_bc, w_step, HEADS)
        for flipped in (False, True):
            result, back = jax.vjp(partial(direction_run, consts=consts, flipped=flipped), inputs)
            normed.append(result)
            local_back.append(back)
    z_main = (normed[0] + normed[1]).astype(jnp.bfloat16)
    z_rc = (normed[2] + normed[3]).astype(jnp.bfloat16)
    out_terms = jnp.dot(z_main, w_out, preferred_element_type=jnp.float32) + jnp.dot(z_rc, w_out, preferred_element_type=jnp.float32)[:, ::-1]
    out = out_terms.astype(jnp.bfloat16)
    known_base = (ids != 4).astype(jnp.bfloat16)[:, None]
    grad = cotangent * known_base
    dz_main = times_transposed(grad, w_out).astype(jnp.bfloat16).astype(jnp.float32)
    dz_rc = times_transposed(grad[:, ::-1], w_out).astype(jnp.bfloat16).astype(jnp.float32)
    grads = [local_back[0](dz_main)[0], local_back[1](dz_main)[0], local_back[2](dz_rc)[0], local_back[3](dz_rc)[0]]
    packed_main = pack_grads(grads[0], grads[1])
    packed_rc = pack_grads(grads[2], grads[3])
    terms = input_terms(packed_main, w_value, w_bc, w_step) + input_terms(packed_rc, w_value, w_bc, w_step)[:, ::-1]
    return (out, terms.astype(jnp.bfloat16))
```

```python
from functools import partial

import jax
import jax.numpy as jnp
from jax import lax
from jax.experimental import pallas as pl
from jax.experimental.pallas import tpu as pltpu
from jax.sharding import PartitionSpec as P

f32, bf16 = jnp.float32, jnp.bfloat16
epsilon = 1e-05
LANES = 128
MXU_NN = (((1,), (0,)), ((), ()))
MXU_NT = (((1,), (1,)), ((), ()))
MXU_TN = (((0,), (0,)), ((), ()))
PARAMS = pltpu.CompilerParams(vmem_limit_bytes=56 * 1024 * 1024)


def dot(a, b, dims=MXU_NN, precision=None):
    return lax.dot_general(a, b, dims, preferred_element_type=f32, precision=precision)


def iota2(shape, axis):
    return lax.broadcasted_iota(jnp.int32, shape, axis)


def exchange_matrix():
    return (iota2((LANES, LANES), 0) + iota2((LANES, LANES), 1) == LANES - 1).astype(bf16)


def sources_kernel(hidden_ref, cot_ref, ids_ref, src_ref, grad_ref):
    tiles = hidden_ref.shape[1] // LANES
    mirror = exchange_matrix()
    known = ids_ref[...] != 4
    src_ref[0] = hidden_ref[...]
    for k in range(tiles):
        there = pl.ds((tiles - 1 - k) * LANES, LANES)
        here = pl.ds(k * LANES, LANES)
        src_ref[1, :, there] = dot(hidden_ref[:, here], mirror).astype(bf16)
        tile = jnp.where(known, cot_ref[:, here].astype(f32), 0.0).astype(bf16)
        grad_ref[0, :, here] = tile
        grad_ref[1, :, there] = dot(tile, mirror).astype(bf16)


def merge_kernel(terms_ref, out_ref):
    parts, _, width = out_ref.shape
    tiles = parts * width // LANES
    per = width // LANES
    mirror = exchange_matrix()
    for k in range(tiles):
        back = tiles - 1 - k
        flipped = dot(terms_ref[1, :, pl.ds(back * LANES, LANES)].astype(bf16), mirror)
        out_ref[k // per, :, pl.ds((k % per) * LANES, LANES)] = (
            terms_ref[0, :, pl.ds(k * LANES, LANES)] + flipped
        )


def prepare(aux, consts):
    length = aux.shape[0]
    shifted = aux + consts[0:1]
    dt = jnp.maximum(shifted, 0.0) + jnp.log1p(jnp.exp(-jnp.abs(shifted)))
    la = -jnp.exp(consts[1:2]) * dt
    lower = (iota2((length, length), 0) >= iota2((length, length), 1)).astype(f32)
    cum = dot(lower, la, precision=lax.Precision.HIGHEST)
    return shifted, dt, la, cum, cum - la


def ends_kernel(heads, state, aux_ref, consts_ref, x_ref, st_ref, dec_ref):
    aux = aux_ref[0]
    length = aux.shape[0]
    _, dt, la, cum, exc = prepare(aux, consts_ref[...])
    cum_t, exc_t, dt_t = cum.T[:heads], exc.T[:heads], dt.T[:heads]
    b_t = aux.astype(bf16).astype(f32).T[LANES - 2 * state : LANES - state]
    end = cum_t[:, length - 1 : length]
    w_f = jnp.exp(end - cum_t) * dt_t
    w_r = jnp.exp(exc_t) * dt_t
    for h in range(heads):
        left = jnp.concatenate([b_t * w_f[h : h + 1], b_t * w_r[h : h + 1]], axis=0).astype(bf16)
        both = dot(left, x_ref[0, :, pl.ds(h * LANES, LANES)]).astype(bf16)
        st_ref[0, 0, h] = both[:state]
        st_ref[0, 1, h] = both[state:]
    dec_ref[0] = jnp.broadcast_to(end, (heads, LANES))


def carried(me, count, all_ref, dec_ref, which, upward):
    shape = all_ref.shape[3:]

    def step(i, total):
        j = (count - 1 - i) if upward else i
        return jnp.exp(dec_ref[j, 0])[:, None, :] * total + all_ref[j, 0, which].astype(f32)

    steps = (count - 1 - me) if upward else me
    return lax.fori_loop(0, steps, step, jnp.zeros(shape, f32))


def outputs_kernel(
    heads, state, count,
    me_ref, aux_ref, consts_ref, x_ref, dz_ref, gain_ref, st_ref, dec_ref,
    z_ref, dy_ref, adj_ref, start_ref, y_scr,
):
    aux, consts = aux_ref[0], consts_ref[...]
    length = aux.shape[0]
    me = me_ref[0]
    _, dt, la, cum, exc = prepare(aux, consts)
    cum_t, exc_t, dt_t = cum.T[:heads], exc.T[:heads], dt.T[:heads]
    end_t = cum_t[:, length - 1 : length]
    rounded = aux.astype(bf16)
    b_m = rounded[:, LANES - 2 * state : LANES - state]
    c_m = rounded[:, LANES - state :]
    c32 = c_m.astype(f32)
    c_t = rounded.astype(f32).T[LANES - state :]
    start_ref[0, 0] = carried(me, count, st_ref, dec_ref, 0, False)
    start_ref[0, 1] = carried(me, count, st_ref, dec_ref, 1, True)
    scores = dot(c_m, b_m, MXU_NT)
    rows, cols = iota2((length, length), 0), iota2((length, length), 1)
    grow_f = jnp.exp(cum)
    grow_r = jnp.exp(cum[length - 1 : length] - exc)
    sq_f = jnp.zeros((length, 1), f32)
    sq_r = jnp.zeros((length, 1), f32)
    for h in range(heads):
        at = pl.ds(h * LANES, LANES)
        one = slice(h, h + 1)
        spread = jnp.where(
            rows >= cols, cum[:, one] - cum_t[one], exc_t[one] - exc[:, one]
        )
        mix = jnp.exp(spread) * scores * dt_t[one]
        low = jnp.where(rows >= cols, mix, 0.0).astype(bf16)
        high = jnp.where(rows <= cols, mix, 0.0).astype(bf16)
        x_h = x_ref[0, :, at]
        direct = consts[2:3, one] * x_h.astype(f32)
        y_f = dot(low, x_h) + direct
        y_f += dot((c32 * grow_f[:, one]).astype(bf16), start_ref[0, 0, h].astype(bf16))
        y_r = dot(high, x_h) + direct
        y_r += dot((c32 * grow_r[:, one]).astype(bf16), start_ref[0, 1, h].astype(bf16))
        y_scr[0, :, at] = y_f
        y_scr[1, :, at] = y_r
        sq_f += jnp.sum(y_f * y_f, axis=1, keepdims=True)
        sq_r += jnp.sum(y_r * y_r, axis=1, keepdims=True)
    share = 1.0 / (heads * LANES)
    rs_f = lax.rsqrt(sq_f * share + epsilon)
    rs_r = lax.rsqrt(sq_r * share + epsilon)
    m_f = jnp.zeros((length, 1), f32)
    m_r = jnp.zeros((length, 1), f32)
    for h in range(heads):
        at = pl.ds(h * LANES, LANES)
        gain = gain_ref[:, at]
        n_f, n_r = y_scr[0, :, at] * rs_f, y_scr[1, :, at] * rs_r
        z_ref[0, :, at] = (n_f * gain + n_r * gain).astype(bf16)
        g = dz_ref[0, :, at].astype(f32) * gain
        m_f += jnp.sum(g * n_f, axis=1, keepdims=True)
        m_r += jnp.sum(g * n_r, axis=1, keepdims=True)
    m_f, m_r = m_f * share, m_r * share
    out_f = jnp.exp(cum_t)
    out_r = jnp.exp(end_t - exc_t)
    for h in range(heads):
        at = pl.ds(h * LANES, LANES)
        one = slice(h, h + 1)
        g = dz_ref[0, :, at].astype(f32) * gain_ref[:, at]
        d_f = (rs_f * (g - y_scr[0, :, at] * rs_f * m_f)).astype(bf16)
        d_r = (rs_r * (g - y_scr[1, :, at] * rs_r * m_r)).astype(bf16)
        dy_ref[0, 0, :, at] = d_f
        dy_ref[0, 1, :, at] = d_r
        adj_ref[0, 0, h] = dot((c_t * out_f[one]).astype(bf16), d_f).astype(bf16)
        adj_ref[0, 1, h] = dot((c_t * out_r[one]).astype(bf16), d_r).astype(bf16)


def grads_kernel(
    heads, state, count,
    me_ref, aux_ref, consts_ref, x_ref, dy_ref, start_ref, own_ref, adj_ref, dec_ref,
    dx_ref, tail_ref, in_scr,
):
    aux, consts = aux_ref[0], consts_ref[...]
    length = aux.shape[0]
    me = me_ref[0]
    shifted, dt, la, cum, exc = prepare(aux, consts)
    cum_t, exc_t = cum.T[:heads], exc.T[:heads]
    end = cum[length - 1 : length]
    rounded = aux.astype(bf16)
    b_m = rounded[:, LANES - 2 * state : LANES - state]
    c_m = rounded[:, LANES - state :]
    b32, c32 = b_m.astype(f32), c_m.astype(f32)
    in_scr[0] = carried(me, count, adj_ref, dec_ref, 0, True)
    in_scr[1] = carried(me, count, adj_ref, dec_ref, 1, False)
    scores_t = dot(b_m, c_m, MXU_NT)
    rows, cols = iota2((length, length), 0), iota2((length, length), 1)
    lane = iota2((length, LANES), 1)
    lane_row = iota2((1, LANES), 1)
    grow_f, grow_r = jnp.exp(cum), jnp.exp(end - exc)
    tail_f, tail_r = jnp.exp(end - cum), jnp.exp(exc)
    end_decay = jnp.exp(end)
    zero = jnp.zeros((length, LANES), f32)
    into_f, into_r = zero, zero
    carry_f, carry_r = zero, zero
    total = jnp.zeros((1, LANES), f32)
    from_f, from_r = [], []
    d_scores = jnp.zeros((length, length), f32)
    d_b = jnp.zeros((length, state), f32)
    d_c = jnp.zeros((length, state), f32)
    for h in range(heads):
        at = pl.ds(h * LANES, LANES)
        one = slice(h, h + 1)
        x_h, d_f, d_r = x_ref[0, :, at], dy_ref[0, 0, :, at], dy_ref[0, 1, :, at]
        s_f, s_r = start_ref[0, 0, h], start_ref[0, 1, h]
        a_f, a_r = in_scr[0, h], in_scr[1, h]
        dt_h = dt[:, one]
        decay = jnp.exp(
            jnp.where(cols >= rows, cum_t[one] - cum[:, one], exc[:, one] - exc_t[one])
        )
        weight = decay * scores_t
        w_f = jnp.where(cols >= rows, weight, 0.0)
        w_r = jnp.where(cols <= rows, weight, 0.0)
        p_f = dot(x_h, d_f, MXU_NT)
        p_r = dot(x_h, d_r, MXU_NT)
        picked = jnp.where(cols >= rows, p_f, 0.0) + jnp.where(cols <= rows, p_r, 0.0)
        d_scores += decay * picked * dt_h
        n_f, n_r = w_f * p_f, w_r * p_r
        from_f.append(jnp.sum(n_f * dt_h, axis=0, keepdims=True))
        from_r.append(jnp.sum(n_r * dt_h, axis=0, keepdims=True))
        in_f = jnp.sum(n_f, axis=1, keepdims=True)
        in_r = jnp.sum(n_r, axis=1, keepdims=True)
        d_u = dot(w_f.astype(bf16), d_f) + dot(w_r.astype(bf16), d_r)
        d_u += dot((b32 * tail_f[:, one]).astype(bf16), a_f.astype(bf16))
        d_u += dot((b32 * tail_r[:, one]).astype(bf16), a_r.astype(bf16))
        v_f = dot(x_h, a_f.astype(bf16), MXU_NT) * tail_f[:, one]
        v_r = dot(x_h, a_r.astype(bf16), MXU_NT) * tail_r[:, one]
        d_b += (v_f + v_r) * dt_h
        in_f += jnp.sum(v_f * b32, axis=1, keepdims=True)
        in_r += jnp.sum(v_r * b32, axis=1, keepdims=True)
        u_f = dot(d_f, s_f.astype(bf16), MXU_NT) * grow_f[:, one]
        u_r = dot(d_r, s_r.astype(bf16), MXU_NT) * grow_r[:, one]
        d_c += u_f + u_r
        c_f = jnp.sum(u_f * c32, axis=1, keepdims=True)
        c_r = jnp.sum(u_r * c32, axis=1, keepdims=True)
        skipped = consts[2:3, one] * (d_f.astype(f32) + d_r.astype(f32))
        dx_ref[0, :, at] = (dt_h * d_u + skipped).astype(bf16)
        into_f = jnp.where(lane == h, in_f, into_f)
        into_r = jnp.where(lane == h, in_r, into_r)
        carry_f = jnp.where(lane == h, c_f, carry_f)
        carry_r = jnp.where(lane == h, c_r, carry_r)
        ending = a_f * (end_decay[:, one] * s_f + own_ref[0, 0, h].astype(f32))
        ending += a_r * (end_decay[:, one] * s_r)
        ended = jnp.sum(jnp.sum(ending, axis=1, keepdims=True), axis=0, keepdims=True)
        ended += jnp.sum(c_r, axis=0, keepdims=True)
        total = jnp.where(lane_row == h, ended, total)
    pad = [jnp.zeros((LANES - heads, length), f32)]
    given_f = jnp.concatenate(from_f + pad, axis=0).T + carry_f
    given_r = jnp.concatenate(from_r + pad, axis=0).T + carry_r
    d_cum = given_f - dt * into_f
    d_exc = dt * into_r - given_r
    upper = (rows <= cols).astype(f32)
    d_la = dot(upper, d_cum + d_exc, precision=lax.Precision.HIGHEST) - d_exc + total
    d_dt = into_f + into_r - jnp.exp(consts[1:2]) * d_la
    d_raw = jnp.where(lane < heads, d_dt * jax.nn.sigmoid(shifted), 0.0)
    d_scores = d_scores.astype(bf16)
    d_b += dot(d_scores, c_m)
    d_c += dot(d_scores, b_m, MXU_TN)
    tail_ref[0] = jnp.concatenate(
        [d_raw[:, : LANES - 2 * state], d_b, d_c], axis=1
    ).astype(bf16)


def by_stream(*shape):
    return pl.BlockSpec((1,) + shape, lambda s: (s,) + (0,) * len(shape))


def gathered(count, *shape):
    return pl.BlockSpec((count, 1) + shape, lambda s: (0, s) + (0,) * len(shape))


def shared(*shape):
    return pl.BlockSpec(shape, lambda s: (0,) * len(shape))


def shape_of(dtype, *shape):
    return jax.ShapeDtypeStruct(shape, dtype)


def join_halves(terms, parts):
    _, length, width = terms.shape
    halves = pl.pallas_call(
        merge_kernel,
        out_shape=shape_of(f32, parts, length, width // parts),
        compiler_params=PARAMS,
    )(terms)
    mine = lax.axis_index("mp")
    own = lax.dynamic_index_in_dim(halves, mine, 0, keepdims=False)
    for hop in range(1, parts):
        there = lax.rem(mine + hop, parts)
        leaving = lax.dynamic_index_in_dim(halves, there, 0, keepdims=False).astype(bf16)
        own += lax.ppermute(
            leaving, "mp", [(i, (i + hop) % parts) for i in range(parts)]
        ).astype(f32)
    return own.astype(bf16)


def per_device(
    hidden, ids, w_value, w_bc, w_step, step_bias, decay_log, skip, norm_gain, w_out, cotangent
):
    length, width = hidden.shape
    heads = w_step.shape[1]
    inner = w_value.shape[1]
    state = w_bc.shape[2] // 2
    assert w_bc.shape[1] == 1 and inner == heads * LANES
    count, parts = lax.axis_size("seq"), lax.axis_size("mp")
    me = lax.axis_index("seq").reshape(1).astype(jnp.int32)
    me_spec = pl.BlockSpec(memory_space=pltpu.SMEM)
    sources, grads = pl.pallas_call(
        sources_kernel,
        out_shape=(shape_of(bf16, 2, length, width),) * 2,
        compiler_params=PARAMS,
    )(hidden, cotangent, ids[:, None])
    sources = sources.reshape(2 * length, width)
    grads = grads.reshape(2 * length, width)
    spare = jnp.zeros((width, LANES - heads - 2 * state), bf16)
    w_side = jnp.concatenate([w_step, spare, w_bc.reshape(width, -1)], axis=1)
    consts = jnp.pad(
        jnp.stack([step_bias, decay_log, skip]), ((0, 5), (0, LANES - heads))
    )
    aux = dot(sources, w_side).reshape(2, length, LANES)
    x = dot(sources, w_value).astype(bf16).reshape(2, length, inner)
    states, decays = pl.pallas_call(
        partial(ends_kernel, heads, state),
        grid=(2,),
        in_specs=[by_stream(length, LANES), shared(8, LANES), by_stream(length, inner)],
        out_specs=[by_stream(2, heads, state, LANES), by_stream(heads, LANES)],
        out_shape=(shape_of(bf16, 2, 2, heads, state, LANES), shape_of(f32, 2, heads, LANES)),
        compiler_params=PARAMS,
    )(aux, consts, x)
    all_states = lax.all_gather(states, "seq")
    all_decays = lax.all_gather(decays, "seq")
    dz = dot(grads, w_out, MXU_NT).astype(bf16).reshape(2, length, inner)
    state_shape = (2, heads, state, LANES)
    z, dy, adjoint, start = pl.pallas_call(
        partial(outputs_kernel, heads, state, count),
        grid=(2,),
        in_specs=[
            me_spec, by_stream(length, LANES), shared(8, LANES), by_stream(length, inner),
            by_stream(length, inner), shared(1, inner), gathered(count, *state_shape),
            gathered(count, heads, LANES),
        ],
        out_specs=[
            by_stream(length, inner), by_stream(2, length, inner), by_stream(*state_shape),
            by_stream(*state_shape),
        ],
        out_shape=(
            shape_of(bf16, 2, length, inner), shape_of(bf16, 2, 2, length, inner),
            shape_of(bf16, 2, *state_shape), shape_of(f32, 2, *state_shape),
        ),
        scratch_shapes=[pltpu.VMEM((2, length, inner), f32)],
        compiler_params=PARAMS,
    )(me, aux, consts, x, dz, norm_gain[None], all_states, all_decays)
    all_adjoint = lax.all_gather(adjoint, "seq")
    out_terms = dot(z.reshape(2 * length, inner), w_out).reshape(2, length, width)
    out = join_halves(out_terms, parts)
    dx, tail = pl.pallas_call(
        partial(grads_kernel, heads, state, count),
        grid=(2,),
        in_specs=[
            me_spec, by_stream(length, LANES), shared(8, LANES), by_stream(length, inner),
            by_stream(2, length, inner), by_stream(*state_shape), by_stream(*state_shape),
            gathered(count, *state_shape), gathered(count, heads, LANES),
        ],
        out_specs=[by_stream(length, inner), by_stream(length, LANES)],
        out_shape=(shape_of(bf16, 2, length, inner), shape_of(bf16, 2, length, LANES)),
        scratch_shapes=[pltpu.VMEM(state_shape, f32)],
        compiler_params=PARAMS,
    )(me, aux, consts, x, dy, start, states, all_adjoint, all_decays)
    terms = dot(dx.reshape(2 * length, inner), w_value, MXU_NT)
    terms += dot(tail.reshape(2 * length, LANES), w_side, MXU_NT)
    d_hidden = join_halves(terms.reshape(2, length, width), parts)
    return (out, d_hidden)


def solution(mesh):
    in_specs = (
        P("seq", None),
        P("seq"),
        P(None, "mp"),
        P(None, "mp", None),
        P(None, "mp"),
        P("mp"),
        P("mp"),
        P("mp"),
        P("mp"),
        P("mp", None),
        P("seq", None),
    )
    out_specs = (P("seq", "mp"), P("seq", "mp"))
    return jax.shard_map(
        per_device, mesh=mesh, in_specs=in_specs, out_specs=out_specs, check_vma=False
    )
```

```python
from functools import partial

import jax
import jax.numpy as jnp
from jax import lax
from jax.experimental import pallas as pl
from jax.experimental.pallas import tpu as pltpu
from jax.sharding import PartitionSpec as P

f32, bf16 = jnp.float32, jnp.bfloat16
epsilon = 1e-05
LANES = 128
MXU_NN = (((1,), (0,)), ((), ()))
MXU_NT = (((1,), (1,)), ((), ()))
MXU_TN = (((0,), (0,)), ((), ()))
PARAMS = pltpu.CompilerParams(vmem_limit_bytes=56 * 1024 * 1024)


def dot(a, b, dims=MXU_NN, precision=None):
    return lax.dot_general(a, b, dims, preferred_element_type=f32, precision=precision)


def iota2(shape, axis):
    return lax.broadcasted_iota(jnp.int32, shape, axis)


def exchange_matrix():
    return (iota2((LANES, LANES), 0) + iota2((LANES, LANES), 1) == LANES - 1).astype(bf16)


def sources_kernel(hidden_ref, cot_ref, ids_ref, src_ref, grad_ref):
    tiles = hidden_ref.shape[1] // LANES
    mirror = exchange_matrix()
    known = ids_ref[...] != 4
    src_ref[0] = hidden_ref[...]
    for k in range(tiles):
        there = pl.ds((tiles - 1 - k) * LANES, LANES)
        here = pl.ds(k * LANES, LANES)
        src_ref[1, :, there] = dot(hidden_ref[:, here], mirror).astype(bf16)
        tile = jnp.where(known, cot_ref[:, here].astype(f32), 0.0).astype(bf16)
        grad_ref[0, :, here] = tile
        grad_ref[1, :, there] = dot(tile, mirror).astype(bf16)


def merge_kernel(terms_ref, out_ref):
    parts, _, width = out_ref.shape
    tiles = parts * width // LANES
    per = width // LANES
    mirror = exchange_matrix()
    for k in range(tiles):
        back = tiles - 1 - k
        flipped = dot(terms_ref[1, :, pl.ds(back * LANES, LANES)].astype(bf16), mirror)
        out_ref[k // per, :, pl.ds((k % per) * LANES, LANES)] = (
            terms_ref[0, :, pl.ds(k * LANES, LANES)] + flipped
        )


def prepare(aux, consts):
    length = aux.shape[0]
    shifted = aux + consts[0:1]
    dt = jnp.maximum(shifted, 0.0) + jnp.log1p(jnp.exp(-jnp.abs(shifted)))
    la = -jnp.exp(consts[1:2]) * dt
    lower = (iota2((length, length), 0) >= iota2((length, length), 1)).astype(f32)
    cum = dot(lower, la, precision=lax.Precision.HIGHEST)
    return shifted, dt, la, cum, cum - la


def put_rows(parcel_ref, h, which, value):
    count, _, _, rows, _ = parcel_ref.shape
    per = value.shape[0] // rows
    for k in range(per):
        parcel_ref[h * per + k, 0, which] = value[k * rows : (k + 1) * rows].astype(bf16)


def put_decay(parcel_ref, h, heads, decay):
    count, _, _, rows, _ = parcel_ref.shape
    per = count // heads
    wide = jnp.broadcast_to(decay, (rows, LANES))
    main = wide.astype(bf16)
    rest = (wide - main.astype(f32)).astype(bf16)
    for k in range(per):
        parcel_ref[h * per + k, 0, 2] = main
        parcel_ref[h * per + k, 0, 3] = rest


def take_rows(parcel_ref, h, heads, which):
    per = parcel_ref.shape[0] // heads
    pieces = [parcel_ref[h * per + k, 0, which].astype(f32) for k in range(per)]
    return jnp.concatenate(pieces, axis=0)


def exchange_kernel(
    upward, parcel_ref, out_ref, got, back, final, send_out, recv_out, send_back, recv_back
):
    count = parcel_ref.shape[0]
    me = lax.axis_index("seq")
    barrier = pltpu.get_barrier_semaphore()
    mesh_id = pl.DeviceIdType.MESH

    def peer_of(hop):
        return lax.rem(me + hop, count)

    def greet(hop, none):
        pl.semaphore_signal(
            barrier, inc=1, device_id={"seq": peer_of(hop)}, device_id_type=mesh_id
        )
        return none

    lax.fori_loop(1, count, greet, 0)
    pl.semaphore_wait(barrier, count - 1)

    def outward(hop):
        return pltpu.make_async_remote_copy(
            src_ref=parcel_ref.at[peer_of(hop)], dst_ref=got.at[me],
            send_sem=send_out.at[hop], recv_sem=recv_out.at[hop],
            device_id={"seq": peer_of(hop)}, device_id_type=mesh_id,
        )

    def homeward(hop):
        return pltpu.make_async_remote_copy(
            src_ref=back.at[peer_of(hop)], dst_ref=final.at[me],
            send_sem=send_back.at[hop], recv_sem=recv_back.at[hop],
            device_id={"seq": peer_of(hop)}, device_id_type=mesh_id,
        )

    def start(copy):
        def step(hop, none):
            copy(hop).start()
            return none

        lax.fori_loop(1, count, step, 0)

    def finish(copy):
        def step(hop, none):
            copy(hop).wait()
            return none

        lax.fori_loop(1, count, step, 0)

    start(outward)
    got[me] = parcel_ref[me]
    finish(outward)
    rows = got.shape[3]
    zero = jnp.zeros((2, rows, LANES), f32)

    def scan(i, totals):
        result = []
        for which in range(2):
            j = count - 1 - i if (which == 1) != upward else i
            total = totals[which]
            back[j, :, which] = total.astype(bf16)
            decay = got[j, :, 2].astype(f32) + got[j, :, 3].astype(f32)
            result.append(decay * total + got[j, :, which].astype(f32))
        return tuple(result)

    lax.fori_loop(0, count, scan, (zero, zero))
    start(homeward)
    final[me] = back[me]
    finish(homeward)
    out_ref[...] = final[...]


def exchange(parcels, upward, collective_id):
    count, streams, _, rows, _ = parcels.shape
    carried = (count, streams, 2, rows, LANES)
    return pl.pallas_call(
        partial(exchange_kernel, upward),
        in_specs=[pl.BlockSpec(memory_space=pltpu.VMEM)],
        out_specs=pl.BlockSpec(memory_space=pltpu.VMEM),
        out_shape=shape_of(bf16, *carried),
        scratch_shapes=[
            pltpu.VMEM(parcels.shape, bf16), pltpu.VMEM(carried, bf16), pltpu.VMEM(carried, bf16),
        ] + [pltpu.SemaphoreType.DMA((count,))] * 4,
        compiler_params=pltpu.CompilerParams(
            collective_id=collective_id, has_side_effects=True,
            vmem_limit_bytes=32 * 1024 * 1024,
        ),
    )(parcels)


def ends_kernel(heads, state, aux_ref, consts_ref, x_ref, st_ref):
    aux = aux_ref[0]
    length = aux.shape[0]
    _, dt, la, cum, exc = prepare(aux, consts_ref[...])
    cum_t, exc_t, dt_t = cum.T[:heads], exc.T[:heads], dt.T[:heads]
    b_t = aux.astype(bf16).astype(f32).T[LANES - 2 * state : LANES - state]
    end = cum_t[:, length - 1 : length]
    w_f = jnp.exp(end - cum_t) * dt_t
    w_r = jnp.exp(exc_t) * dt_t
    for h in range(heads):
        left = jnp.concatenate([b_t * w_f[h : h + 1], b_t * w_r[h : h + 1]], axis=0).astype(bf16)
        both = dot(left, x_ref[0, :, pl.ds(h * LANES, LANES)])
        put_rows(st_ref, h, 0, both[:state])
        put_rows(st_ref, h, 1, both[state:])
        put_decay(st_ref, h, heads, jnp.exp(end[h : h + 1]))


def outputs_kernel(
    heads, state,
    aux_ref, consts_ref, x_ref, dz_ref, gain_ref, start_ref,
    z_ref, dy_ref, adj_ref, y_scr,
):
    aux, consts = aux_ref[0], consts_ref[...]
    length = aux.shape[0]
    _, dt, la, cum, exc = prepare(aux, consts)
    cum_t, exc_t, dt_t = cum.T[:heads], exc.T[:heads], dt.T[:heads]
    end_t = cum_t[:, length - 1 : length]
    rounded = aux.astype(bf16)
    b_m = rounded[:, LANES - 2 * state : LANES - state]
    c_m = rounded[:, LANES - state :]
    c32 = c_m.astype(f32)
    c_t = rounded.astype(f32).T[LANES - state :]
    scores = dot(c_m, b_m, MXU_NT)
    rows, cols = iota2((length, length), 0), iota2((length, length), 1)
    grow_f = jnp.exp(cum)
    grow_r = jnp.exp(cum[length - 1 : length] - exc)
    sq_f = jnp.zeros((length, 1), f32)
    sq_r = jnp.zeros((length, 1), f32)
    for h in range(heads):
        at = pl.ds(h * LANES, LANES)
        one = slice(h, h + 1)
        spread = jnp.where(
            rows >= cols, cum[:, one] - cum_t[one], exc_t[one] - exc[:, one]
        )
        mix = jnp.exp(spread) * scores * dt_t[one]
        low = jnp.where(rows >= cols, mix, 0.0).astype(bf16)
        high = jnp.where(rows <= cols, mix, 0.0).astype(bf16)
        x_h = x_ref[0, :, at]
        direct = consts[2:3, one] * x_h.astype(f32)
        y_f = dot(low, x_h) + direct
        y_f += dot((c32 * grow_f[:, one]).astype(bf16), take_rows(start_ref, h, heads, 0).astype(bf16))
        y_r = dot(high, x_h) + direct
        y_r += dot((c32 * grow_r[:, one]).astype(bf16), take_rows(start_ref, h, heads, 1).astype(bf16))
        y_scr[0, :, at] = y_f
        y_scr[1, :, at] = y_r
        sq_f += jnp.sum(y_f * y_f, axis=1, keepdims=True)
        sq_r += jnp.sum(y_r * y_r, axis=1, keepdims=True)
    share = 1.0 / (heads * LANES)
    rs_f = lax.rsqrt(sq_f * share + epsilon)
    rs_r = lax.rsqrt(sq_r * share + epsilon)
    m_f = jnp.zeros((length, 1), f32)
    m_r = jnp.zeros((length, 1), f32)
    for h in range(heads):
        at = pl.ds(h * LANES, LANES)
        gain = gain_ref[:, at]
        n_f, n_r = y_scr[0, :, at] * rs_f, y_scr[1, :, at] * rs_r
        z_ref[0, :, at] = (n_f * gain + n_r * gain).astype(bf16)
        g = dz_ref[0, :, at].astype(f32) * gain
        m_f += jnp.sum(g * n_f, axis=1, keepdims=True)
        m_r += jnp.sum(g * n_r, axis=1, keepdims=True)
    m_f, m_r = m_f * share, m_r * share
    out_f = jnp.exp(cum_t)
    out_r = jnp.exp(end_t - exc_t)
    for h in range(heads):
        at = pl.ds(h * LANES, LANES)
        one = slice(h, h + 1)
        g = dz_ref[0, :, at].astype(f32) * gain_ref[:, at]
        d_f = (rs_f * (g - y_scr[0, :, at] * rs_f * m_f)).astype(bf16)
        d_r = (rs_r * (g - y_scr[1, :, at] * rs_r * m_r)).astype(bf16)
        dy_ref[0, 0, :, at] = d_f
        dy_ref[0, 1, :, at] = d_r
        put_rows(adj_ref, h, 0, dot((c_t * out_f[one]).astype(bf16), d_f))
        put_rows(adj_ref, h, 1, dot((c_t * out_r[one]).astype(bf16), d_r))
        put_decay(adj_ref, h, heads, jnp.exp(end_t[one]))


def grads_kernel(
    heads, state,
    aux_ref, consts_ref, x_ref, dy_ref, start_ref, own_ref, in_ref,
    dx_ref, tail_ref,
):
    aux, consts = aux_ref[0], consts_ref[...]
    length = aux.shape[0]
    shifted, dt, la, cum, exc = prepare(aux, consts)
    cum_t, exc_t = cum.T[:heads], exc.T[:heads]
    end = cum[length - 1 : length]
    rounded = aux.astype(bf16)
    b_m = rounded[:, LANES - 2 * state : LANES - state]
    c_m = rounded[:, LANES - state :]
    b32, c32 = b_m.astype(f32), c_m.astype(f32)
    scores_t = dot(b_m, c_m, MXU_NT)
    rows, cols = iota2((length, length), 0), iota2((length, length), 1)
    lane = iota2((length, LANES), 1)
    lane_row = iota2((1, LANES), 1)
    grow_f, grow_r = jnp.exp(cum), jnp.exp(end - exc)
    tail_f, tail_r = jnp.exp(end - cum), jnp.exp(exc)
    end_decay = jnp.exp(end)
    zero = jnp.zeros((length, LANES), f32)
    into_f, into_r = zero, zero
    carry_f, carry_r = zero, zero
    total = jnp.zeros((1, LANES), f32)
    from_f, from_r = [], []
    d_scores = jnp.zeros((length, length), f32)
    d_b = jnp.zeros((length, state), f32)
    d_c = jnp.zeros((length, state), f32)
    for h in range(heads):
        at = pl.ds(h * LANES, LANES)
        one = slice(h, h + 1)
        x_h, d_f, d_r = x_ref[0, :, at], dy_ref[0, 0, :, at], dy_ref[0, 1, :, at]
        s_f, s_r = take_rows(start_ref, h, heads, 0), take_rows(start_ref, h, heads, 1)
        a_f, a_r = take_rows(in_ref, h, heads, 0), take_rows(in_ref, h, heads, 1)
        dt_h = dt[:, one]
        decay = jnp.exp(
            jnp.where(cols >= rows, cum_t[one] - cum[:, one], exc[:, one] - exc_t[one])
        )
        weight = decay * scores_t
        w_f = jnp.where(cols >= rows, weight, 0.0)
        w_r = jnp.where(cols <= rows, weight, 0.0)
        p_f = dot(x_h, d_f, MXU_NT)
        p_r = dot(x_h, d_r, MXU_NT)
        picked = jnp.where(cols >= rows, p_f, 0.0) + jnp.where(cols <= rows, p_r, 0.0)
        d_scores += decay * picked * dt_h
        n_f, n_r = w_f * p_f, w_r * p_r
        from_f.append(jnp.sum(n_f * dt_h, axis=0, keepdims=True))
        from_r.append(jnp.sum(n_r * dt_h, axis=0, keepdims=True))
        in_f = jnp.sum(n_f, axis=1, keepdims=True)
        in_r = jnp.sum(n_r, axis=1, keepdims=True)
        d_u = dot(w_f.astype(bf16), d_f) + dot(w_r.astype(bf16), d_r)
        d_u += dot((b32 * tail_f[:, one]).astype(bf16), a_f.astype(bf16))
        d_u += dot((b32 * tail_r[:, one]).astype(bf16), a_r.astype(bf16))
        v_f = dot(x_h, a_f.astype(bf16), MXU_NT) * tail_f[:, one]
        v_r = dot(x_h, a_r.astype(bf16), MXU_NT) * tail_r[:, one]
        d_b += (v_f + v_r) * dt_h
        in_f += jnp.sum(v_f * b32, axis=1, keepdims=True)
        in_r += jnp.sum(v_r * b32, axis=1, keepdims=True)
        u_f = dot(d_f, s_f.astype(bf16), MXU_NT) * grow_f[:, one]
        u_r = dot(d_r, s_r.astype(bf16), MXU_NT) * grow_r[:, one]
        d_c += u_f + u_r
        c_f = jnp.sum(u_f * c32, axis=1, keepdims=True)
        c_r = jnp.sum(u_r * c32, axis=1, keepdims=True)
        skipped = consts[2:3, one] * (d_f.astype(f32) + d_r.astype(f32))
        dx_ref[0, :, at] = (dt_h * d_u + skipped).astype(bf16)
        into_f = jnp.where(lane == h, in_f, into_f)
        into_r = jnp.where(lane == h, in_r, into_r)
        carry_f = jnp.where(lane == h, c_f, carry_f)
        carry_r = jnp.where(lane == h, c_r, carry_r)
        ending = a_f * (end_decay[:, one] * s_f + take_rows(own_ref, h, heads, 0))
        ending += a_r * (end_decay[:, one] * s_r)
        ended = jnp.sum(jnp.sum(ending, axis=1, keepdims=True), axis=0, keepdims=True)
        ended += jnp.sum(c_r, axis=0, keepdims=True)
        total = jnp.where(lane_row == h, ended, total)
    pad = [jnp.zeros((LANES - heads, length), f32)]
    given_f = jnp.concatenate(from_f + pad, axis=0).T + carry_f
    given_r = jnp.concatenate(from_r + pad, axis=0).T + carry_r
    d_cum = given_f - dt * into_f
    d_exc = dt * into_r - given_r
    upper = (rows <= cols).astype(f32)
    d_la = dot(upper, d_cum + d_exc, precision=lax.Precision.HIGHEST) - d_exc + total
    d_dt = into_f + into_r - jnp.exp(consts[1:2]) * d_la
    d_raw = jnp.where(lane < heads, d_dt * jax.nn.sigmoid(shifted), 0.0)
    d_scores = d_scores.astype(bf16)
    d_b += dot(d_scores, c_m)
    d_c += dot(d_scores, b_m, MXU_TN)
    tail_ref[0] = jnp.concatenate(
        [d_raw[:, : LANES - 2 * state], d_b, d_c], axis=1
    ).astype(bf16)


def by_stream(*shape):
    return pl.BlockSpec((1,) + shape, lambda s: (s,) + (0,) * len(shape))


def gathered(count, *shape):
    return pl.BlockSpec((count, 1) + shape, lambda s: (0, s) + (0,) * len(shape))


def shared(*shape):
    return pl.BlockSpec(shape, lambda s: (0,) * len(shape))


def shape_of(dtype, *shape):
    return jax.ShapeDtypeStruct(shape, dtype)


def join_halves(terms, parts):
    _, length, width = terms.shape
    halves = pl.pallas_call(
        merge_kernel,
        out_shape=shape_of(f32, parts, length, width // parts),
        compiler_params=PARAMS,
    )(terms)
    mine = lax.axis_index("mp")
    own = lax.dynamic_index_in_dim(halves, mine, 0, keepdims=False)
    for hop in range(1, parts):
        there = lax.rem(mine + hop, parts)
        leaving = lax.dynamic_index_in_dim(halves, there, 0, keepdims=False).astype(bf16)
        own += lax.ppermute(
            leaving, "mp", [(i, (i + hop) % parts) for i in range(parts)]
        ).astype(f32)
    return own.astype(bf16)


def per_device(
    hidden, ids, w_value, w_bc, w_step, step_bias, decay_log, skip, norm_gain, w_out, cotangent
):
    length, width = hidden.shape
    heads = w_step.shape[1]
    inner = w_value.shape[1]
    state = w_bc.shape[2] // 2
    assert w_bc.shape[1] == 1 and inner == heads * LANES
    count, parts = lax.axis_size("seq"), lax.axis_size("mp")
    sources, grads = pl.pallas_call(
        sources_kernel,
        out_shape=(shape_of(bf16, 2, length, width),) * 2,
        compiler_params=PARAMS,
    )(hidden, cotangent, ids[:, None])
    sources = sources.reshape(2 * length, width)
    grads = grads.reshape(2 * length, width)
    spare = jnp.zeros((width, LANES - heads - 2 * state), bf16)
    w_side = jnp.concatenate([w_step, spare, w_bc.reshape(width, -1)], axis=1)
    consts = jnp.pad(
        jnp.stack([step_bias, decay_log, skip]), ((0, 5), (0, LANES - heads))
    )
    aux = dot(sources, w_side).reshape(2, length, LANES)
    x = dot(sources, w_value).astype(bf16).reshape(2, length, inner)
    assert count % heads == 0 and (heads * state) % count == 0
    rows = heads * state // count
    parcel = (count, 2, 4, rows, LANES)
    states = pl.pallas_call(
        partial(ends_kernel, heads, state),
        grid=(2,),
        in_specs=[by_stream(length, LANES), shared(8, LANES), by_stream(length, inner)],
        out_specs=gathered(count, 4, rows, LANES),
        out_shape=shape_of(bf16, *parcel),
        compiler_params=PARAMS,
    )(aux, consts, x)
    starts = exchange(states, False, 0)
    dz = dot(grads, w_out, MXU_NT).astype(bf16).reshape(2, length, inner)
    z, dy, adjoint = pl.pallas_call(
        partial(outputs_kernel, heads, state),
        grid=(2,),
        in_specs=[
            by_stream(length, LANES), shared(8, LANES), by_stream(length, inner),
            by_stream(length, inner), shared(1, inner), gathered(count, 2, rows, LANES),
        ],
        out_specs=[
            by_stream(length, inner), by_stream(2, length, inner),
            gathered(count, 4, rows, LANES),
        ],
        out_shape=(
            shape_of(bf16, 2, length, inner), shape_of(bf16, 2, 2, length, inner),
            shape_of(bf16, *parcel),
        ),
        scratch_shapes=[pltpu.VMEM((2, length, inner), f32)],
        compiler_params=PARAMS,
    )(aux, consts, x, dz, norm_gain[None], starts)
    out_terms = dot(z.reshape(2 * length, inner), w_out).reshape(2, length, width)
    out = join_halves(out_terms, parts)
    arriving = exchange(adjoint, True, 1)
    dx, tail = pl.pallas_call(
        partial(grads_kernel, heads, state),
        grid=(2,),
        in_specs=[
            by_stream(length, LANES), shared(8, LANES), by_stream(length, inner),
            by_stream(2, length, inner), gathered(count, 2, rows, LANES),
            gathered(count, 4, rows, LANES), gathered(count, 2, rows, LANES),
        ],
        out_specs=[by_stream(length, inner), by_stream(length, LANES)],
        out_shape=(shape_of(bf16, 2, length, inner), shape_of(bf16, 2, length, LANES)),
        compiler_params=PARAMS,
    )(aux, consts, x, dy, starts, states, arriving)
    terms = dot(dx.reshape(2 * length, inner), w_value, MXU_NT)
    terms += dot(tail.reshape(2 * length, LANES), w_side, MXU_NT)
    d_hidden = join_halves(terms.reshape(2, length, width), parts)
    return (out, d_hidden)


def solution(mesh):
    in_specs = (
        P("seq", None),
        P("seq"),
        P(None, "mp"),
        P(None, "mp", None),
        P(None, "mp"),
        P("mp"),
        P("mp"),
        P("mp"),
        P("mp"),
        P("mp", None),
        P("seq", None),
    )
    out_specs = (P("seq", "mp"), P("seq", "mp"))
    return jax.shard_map(
        per_device, mesh=mesh, in_specs=in_specs, out_specs=out_specs, check_vma=False
    )
```

```python
from functools import partial

import jax
import jax.numpy as jnp
from jax import lax
from jax.experimental import pallas as pl
from jax.experimental.pallas import tpu as pltpu
from jax.sharding import PartitionSpec as P

f32, bf16 = jnp.float32, jnp.bfloat16
epsilon = 1e-05
LANES = 128
MXU_NN = (((1,), (0,)), ((), ()))
MXU_NT = (((1,), (1,)), ((), ()))
MXU_TN = (((0,), (0,)), ((), ()))
PARAMS = pltpu.CompilerParams(vmem_limit_bytes=56 * 1024 * 1024)


def dot(a, b, dims=MXU_NN, precision=None):
    return lax.dot_general(a, b, dims, preferred_element_type=f32, precision=precision)


def iota2(shape, axis):
    return lax.broadcasted_iota(jnp.int32, shape, axis)


def exchange_matrix():
    return (iota2((LANES, LANES), 0) + iota2((LANES, LANES), 1) == LANES - 1).astype(bf16)


def sources_kernel(hidden_ref, cot_ref, ids_ref, src_ref, grad_ref):
    tiles = hidden_ref.shape[1] // LANES
    mirror = exchange_matrix()
    known = ids_ref[...] != 4
    src_ref[0] = hidden_ref[...]
    for k in range(tiles):
        there = pl.ds((tiles - 1 - k) * LANES, LANES)
        here = pl.ds(k * LANES, LANES)
        src_ref[1, :, there] = dot(hidden_ref[:, here], mirror).astype(bf16)
        tile = jnp.where(known, cot_ref[:, here].astype(f32), 0.0).astype(bf16)
        grad_ref[0, :, here] = tile
        grad_ref[1, :, there] = dot(tile, mirror).astype(bf16)


def merge_kernel(main_ref, mirrored_ref, out_ref):
    tiles = out_ref.shape[1] // LANES
    mirror = exchange_matrix()
    for k in range(tiles):
        here = pl.ds(k * LANES, LANES)
        there = pl.ds((tiles - 1 - k) * LANES, LANES)
        flipped = dot(mirrored_ref[:, there].astype(bf16), mirror)
        out_ref[:, here] = (main_ref[:, here] + flipped).astype(out_ref.dtype)


def prepare(aux, consts):
    length = aux.shape[0]
    shifted = aux + consts[0:1]
    dt = jnp.maximum(shifted, 0.0) + jnp.log1p(jnp.exp(-jnp.abs(shifted)))
    la = -jnp.exp(consts[1:2]) * dt
    lower = (iota2((length, length), 0) >= iota2((length, length), 1)).astype(f32)
    cum = dot(lower, la, precision=lax.Precision.HIGHEST)
    return shifted, dt, la, cum, cum - la


def put_rows(parcel_ref, h, which, value):
    count, _, _, rows, _ = parcel_ref.shape
    per = value.shape[0] // rows
    for k in range(per):
        parcel_ref[h * per + k, 0, which] = value[k * rows : (k + 1) * rows].astype(bf16)


def put_decay(parcel_ref, h, heads, decay):
    count, _, _, rows, _ = parcel_ref.shape
    per = count // heads
    wide = jnp.broadcast_to(decay, (rows, LANES))
    main = wide.astype(bf16).astype(f32)
    packed = jnp.where(iota2((rows, LANES), 0) < rows // 2, main, wide - main).astype(bf16)
    for k in range(per):
        parcel_ref[h * per + k, 0, 2] = packed


def take_rows(parcel_ref, h, heads, which):
    per = parcel_ref.shape[0] // heads
    pieces = [parcel_ref[h * per + k, 0, which].astype(f32) for k in range(per)]
    return jnp.concatenate(pieces, axis=0)


def exchange_kernel(
    upward, parcel_ref, out_ref, got, back, final, send_out, recv_out, send_back, recv_back
):
    count = parcel_ref.shape[0]
    me = lax.axis_index("seq")
    barrier = pltpu.get_barrier_semaphore()
    mesh_id = pl.DeviceIdType.MESH

    def peer_of(hop):
        return lax.rem(me + hop, count)

    def greet(hop, none):
        pl.semaphore_signal(
            barrier, inc=1, device_id={"seq": peer_of(hop)}, device_id_type=mesh_id
        )
        return none

    lax.fori_loop(1, count, greet, 0)
    pl.semaphore_wait(barrier, count - 1)

    def outward(hop):
        return pltpu.make_async_remote_copy(
            src_ref=parcel_ref.at[peer_of(hop)], dst_ref=got.at[me],
            send_sem=send_out.at[hop], recv_sem=recv_out.at[hop],
            device_id={"seq": peer_of(hop)}, device_id_type=mesh_id,
        )

    def homeward(hop):
        return pltpu.make_async_remote_copy(
            src_ref=back.at[peer_of(hop)], dst_ref=final.at[me],
            send_sem=send_back.at[hop], recv_sem=recv_back.at[hop],
            device_id={"seq": peer_of(hop)}, device_id_type=mesh_id,
        )

    def start(copy):
        def step(hop, none):
            copy(hop).start()
            return none

        lax.fori_loop(1, count, step, 0)

    def finish(copy):
        def step(hop, none):
            copy(hop).wait()
            return none

        lax.fori_loop(1, count, step, 0)

    start(outward)
    got[me] = parcel_ref[me]
    finish(outward)
    rows = got.shape[3]
    zero = jnp.zeros((2, rows, LANES), f32)

    def scan(i, totals):
        result = []
        for which in range(2):
            j = count - 1 - i if (which == 1) != upward else i
            total = totals[which]
            back[j, :, which] = total.astype(bf16)
            packed = got[j, :, 2].astype(f32)
            decay = packed[:, :1] + packed[:, rows // 2 : rows // 2 + 1]
            result.append(decay * total + got[j, :, which].astype(f32))
        return tuple(result)

    lax.fori_loop(0, count, scan, (zero, zero))
    start(homeward)
    final[me] = back[me]
    finish(homeward)
    out_ref[...] = final[...]


def exchange(parcels, upward, collective_id):
    count, streams, _, rows, _ = parcels.shape
    carried = (count, streams, 2, rows, LANES)
    return pl.pallas_call(
        partial(exchange_kernel, upward),
        in_specs=[pl.BlockSpec(memory_space=pltpu.VMEM)],
        out_specs=pl.BlockSpec(memory_space=pltpu.VMEM),
        out_shape=shape_of(bf16, *carried),
        scratch_shapes=[
            pltpu.VMEM(parcels.shape, bf16), pltpu.VMEM(carried, bf16), pltpu.VMEM(carried, bf16),
        ] + [pltpu.SemaphoreType.DMA((count,))] * 4,
        compiler_params=pltpu.CompilerParams(
            collective_id=collective_id, has_side_effects=True,
            vmem_limit_bytes=32 * 1024 * 1024,
        ),
    )(parcels)


def ends_kernel(heads, state, aux_ref, consts_ref, x_ref, st_ref):
    aux = aux_ref[0]
    length = aux.shape[0]
    _, dt, la, cum, exc = prepare(aux, consts_ref[...])
    cum_t, exc_t, dt_t = cum.T[:heads], exc.T[:heads], dt.T[:heads]
    b_t = aux.astype(bf16).astype(f32).T[LANES - 2 * state : LANES - state]
    end = cum_t[:, length - 1 : length]
    w_f = jnp.exp(end - cum_t) * dt_t
    w_r = jnp.exp(exc_t) * dt_t
    for h in range(heads):
        left = jnp.concatenate([b_t * w_f[h : h + 1], b_t * w_r[h : h + 1]], axis=0).astype(bf16)
        both = dot(left, x_ref[0, :, pl.ds(h * LANES, LANES)])
        put_rows(st_ref, h, 0, both[:state])
        put_rows(st_ref, h, 1, both[state:])
        put_decay(st_ref, h, heads, jnp.exp(end[h : h + 1]))


def outputs_kernel(
    heads, state,
    aux_ref, consts_ref, x_ref, dz_ref, gain_ref, start_ref,
    z_ref, dy_ref, adj_ref, y_scr,
):
    aux, consts = aux_ref[0], consts_ref[...]
    length = aux.shape[0]
    _, dt, la, cum, exc = prepare(aux, consts)
    cum_t, exc_t, dt_t = cum.T[:heads], exc.T[:heads], dt.T[:heads]
    end_t = cum_t[:, length - 1 : length]
    rounded = aux.astype(bf16)
    b_m = rounded[:, LANES - 2 * state : LANES - state]
    c_m = rounded[:, LANES - state :]
    c32 = c_m.astype(f32)
    c_t = rounded.astype(f32).T[LANES - state :]
    scores = dot(c_m, b_m, MXU_NT)
    rows, cols = iota2((length, length), 0), iota2((length, length), 1)
    grow_f = jnp.exp(cum)
    grow_r = jnp.exp(cum[length - 1 : length] - exc)
    sq_f = jnp.zeros((length, 1), f32)
    sq_r = jnp.zeros((length, 1), f32)
    for h in range(heads):
        at = pl.ds(h * LANES, LANES)
        one = slice(h, h + 1)
        spread = jnp.where(
            rows >= cols, cum[:, one] - cum_t[one], exc_t[one] - exc[:, one]
        )
        mix = jnp.exp(spread) * scores * dt_t[one]
        low = jnp.where(rows >= cols, mix, 0.0).astype(bf16)
        high = jnp.where(rows <= cols, mix, 0.0).astype(bf16)
        x_h = x_ref[0, :, at]
        direct = consts[2:3, one] * x_h.astype(f32)
        y_f = dot(low, x_h) + direct
        y_f += dot((c32 * grow_f[:, one]).astype(bf16), take_rows(start_ref, h, heads, 0).astype(bf16))
        y_r = dot(high, x_h) + direct
        y_r += dot((c32 * grow_r[:, one]).astype(bf16), take_rows(start_ref, h, heads, 1).astype(bf16))
        y_scr[0, :, at] = y_f
        y_scr[1, :, at] = y_r
        sq_f += jnp.sum(y_f * y_f, axis=1, keepdims=True)
        sq_r += jnp.sum(y_r * y_r, axis=1, keepdims=True)
    share = 1.0 / (heads * LANES)
    rs_f = lax.rsqrt(sq_f * share + epsilon)
    rs_r = lax.rsqrt(sq_r * share + epsilon)
    m_f = jnp.zeros((length, 1), f32)
    m_r = jnp.zeros((length, 1), f32)
    for h in range(heads):
        at = pl.ds(h * LANES, LANES)
        gain = gain_ref[:, at]
        n_f, n_r = y_scr[0, :, at] * rs_f, y_scr[1, :, at] * rs_r
        z_ref[0, :, at] = (n_f * gain + n_r * gain).astype(bf16)
        g = dz_ref[0, :, at].astype(f32) * gain
        m_f += jnp.sum(g * n_f, axis=1, keepdims=True)
        m_r += jnp.sum(g * n_r, axis=1, keepdims=True)
    m_f, m_r = m_f * share, m_r * share
    out_f = jnp.exp(cum_t)
    out_r = jnp.exp(end_t - exc_t)
    for h in range(heads):
        at = pl.ds(h * LANES, LANES)
        one = slice(h, h + 1)
        g = dz_ref[0, :, at].astype(f32) * gain_ref[:, at]
        d_f = (rs_f * (g - y_scr[0, :, at] * rs_f * m_f)).astype(bf16)
        d_r = (rs_r * (g - y_scr[1, :, at] * rs_r * m_r)).astype(bf16)
        dy_ref[0, 0, :, at] = d_f
        dy_ref[0, 1, :, at] = d_r
        put_rows(adj_ref, h, 0, dot((c_t * out_f[one]).astype(bf16), d_f))
        put_rows(adj_ref, h, 1, dot((c_t * out_r[one]).astype(bf16), d_r))
        put_decay(adj_ref, h, heads, jnp.exp(end_t[one]))


def grads_kernel(
    heads, state,
    aux_ref, consts_ref, x_ref, dy_ref, start_ref, own_ref, in_ref,
    dx_ref, tail_ref,
):
    aux, consts = aux_ref[0], consts_ref[...]
    length = aux.shape[0]
    shifted, dt, la, cum, exc = prepare(aux, consts)
    cum_t, exc_t = cum.T[:heads], exc.T[:heads]
    end = cum[length - 1 : length]
    rounded = aux.astype(bf16)
    b_m = rounded[:, LANES - 2 * state : LANES - state]
    c_m = rounded[:, LANES - state :]
    b32, c32 = b_m.astype(f32), c_m.astype(f32)
    scores_t = dot(b_m, c_m, MXU_NT)
    rows, cols = iota2((length, length), 0), iota2((length, length), 1)
    lane = iota2((length, LANES), 1)
    lane_row = iota2((1, LANES), 1)
    grow_f, grow_r = jnp.exp(cum), jnp.exp(end - exc)
    tail_f, tail_r = jnp.exp(end - cum), jnp.exp(exc)
    end_decay = jnp.exp(end)
    zero = jnp.zeros((length, LANES), f32)
    into_f, into_r = zero, zero
    carry_f, carry_r = zero, zero
    total = jnp.zeros((1, LANES), f32)
    from_f, from_r = [], []
    d_scores = jnp.zeros((length, length), f32)
    d_b = jnp.zeros((length, state), f32)
    d_c = jnp.zeros((length, state), f32)
    for h in range(heads):
        at = pl.ds(h * LANES, LANES)
        one = slice(h, h + 1)
        x_h, d_f, d_r = x_ref[0, :, at], dy_ref[0, 0, :, at], dy_ref[0, 1, :, at]
        s_f, s_r = take_rows(start_ref, h, heads, 0), take_rows(start_ref, h, heads, 1)
        a_f, a_r = take_rows(in_ref, h, heads, 0), take_rows(in_ref, h, heads, 1)
        dt_h = dt[:, one]
        decay = jnp.exp(
            jnp.where(cols >= rows, cum_t[one] - cum[:, one], exc[:, one] - exc_t[one])
        )
        weight = decay * scores_t
        w_f = jnp.where(cols >= rows, weight, 0.0)
        w_r = jnp.where(cols <= rows, weight, 0.0)
        p_f = dot(x_h, d_f, MXU_NT)
        p_r = dot(x_h, d_r, MXU_NT)
        picked = jnp.where(cols >= rows, p_f, 0.0) + jnp.where(cols <= rows, p_r, 0.0)
        d_scores += decay * picked * dt_h
        n_f, n_r = w_f * p_f, w_r * p_r
        from_f.append(jnp.sum(n_f * dt_h, axis=0, keepdims=True))
        from_r.append(jnp.sum(n_r * dt_h, axis=0, keepdims=True))
        in_f = jnp.sum(n_f, axis=1, keepdims=True)
        in_r = jnp.sum(n_r, axis=1, keepdims=True)
        d_u = dot(w_f.astype(bf16), d_f) + dot(w_r.astype(bf16), d_r)
        d_u += dot((b32 * tail_f[:, one]).astype(bf16), a_f.astype(bf16))
        d_u += dot((b32 * tail_r[:, one]).astype(bf16), a_r.astype(bf16))
        v_f = dot(x_h, a_f.astype(bf16), MXU_NT) * tail_f[:, one]
        v_r = dot(x_h, a_r.astype(bf16), MXU_NT) * tail_r[:, one]
        d_b += (v_f + v_r) * dt_h
        in_f += jnp.sum(v_f * b32, axis=1, keepdims=True)
        in_r += jnp.sum(v_r * b32, axis=1, keepdims=True)
        u_f = dot(d_f, s_f.astype(bf16), MXU_NT) * grow_f[:, one]
        u_r = dot(d_r, s_r.astype(bf16), MXU_NT) * grow_r[:, one]
        d_c += u_f + u_r
        c_f = jnp.sum(u_f * c32, axis=1, keepdims=True)
        c_r = jnp.sum(u_r * c32, axis=1, keepdims=True)
        skipped = consts[2:3, one] * (d_f.astype(f32) + d_r.astype(f32))
        dx_ref[0, :, at] = (dt_h * d_u + skipped).astype(bf16)
        into_f = jnp.where(lane == h, in_f, into_f)
        into_r = jnp.where(lane == h, in_r, into_r)
        carry_f = jnp.where(lane == h, c_f, carry_f)
        carry_r = jnp.where(lane == h, c_r, carry_r)
        ending = a_f * (end_decay[:, one] * s_f + take_rows(own_ref, h, heads, 0))
        ending += a_r * (end_decay[:, one] * s_r)
        ended = jnp.sum(jnp.sum(ending, axis=1, keepdims=True), axis=0, keepdims=True)
        ended += jnp.sum(c_r, axis=0, keepdims=True)
        total = jnp.where(lane_row == h, ended, total)
    pad = [jnp.zeros((LANES - heads, length), f32)]
    given_f = jnp.concatenate(from_f + pad, axis=0).T + carry_f
    given_r = jnp.concatenate(from_r + pad, axis=0).T + carry_r
    d_cum = given_f - dt * into_f
    d_exc = dt * into_r - given_r
    upper = (rows <= cols).astype(f32)
    d_la = dot(upper, d_cum + d_exc, precision=lax.Precision.HIGHEST) - d_exc + total
    d_dt = into_f + into_r - jnp.exp(consts[1:2]) * d_la
    d_raw = jnp.where(lane < heads, d_dt * jax.nn.sigmoid(shifted), 0.0)
    d_scores = d_scores.astype(bf16)
    d_b += dot(d_scores, c_m)
    d_c += dot(d_scores, b_m, MXU_TN)
    tail_ref[0] = jnp.concatenate(
        [d_raw[:, : LANES - 2 * state], d_b, d_c], axis=1
    ).astype(bf16)


def by_stream(*shape):
    return pl.BlockSpec((1,) + shape, lambda s: (s,) + (0,) * len(shape))


def gathered(count, *shape):
    return pl.BlockSpec((count, 1) + shape, lambda s: (0, s) + (0,) * len(shape))


def shared(*shape):
    return pl.BlockSpec(shape, lambda s: (0,) * len(shape))


def shape_of(dtype, *shape):
    return jax.ShapeDtypeStruct(shape, dtype)


def merge(main, mirrored, dtype):
    return pl.pallas_call(
        merge_kernel, out_shape=shape_of(dtype, *main.shape), compiler_params=PARAMS
    )(main, mirrored)


def out_share(z, w_out, part, parts, dtype):
    width = w_out.shape[1] // parts
    main = lax.dynamic_slice_in_dim(w_out, part * width, width, 1)
    mirrored = lax.dynamic_slice_in_dim(w_out, (parts - 1 - part) * width, width, 1)
    return merge(dot(z[0], main), dot(z[1], mirrored), dtype)


def hidden_share(dx, tail, w_value, w_side, part, parts, dtype):
    width = w_value.shape[0] // parts
    terms = []
    for stream, place in ((0, part), (1, parts - 1 - part)):
        value = lax.dynamic_slice_in_dim(w_value, place * width, width, 0)
        side = lax.dynamic_slice_in_dim(w_side, place * width, width, 0)
        terms.append(dot(dx[stream], value, MXU_NT) + dot(tail[stream], side, MXU_NT))
    return merge(*terms, dtype)


def send_on(leaving, hop, parts):
    return lax.ppermute(leaving, "mp", [(i, (i + hop) % parts) for i in range(parts)])


def per_device(
    hidden, ids, w_value, w_bc, w_step, step_bias, decay_log, skip, norm_gain, w_out, cotangent
):
    length, width = hidden.shape
    heads = w_step.shape[1]
    inner = w_value.shape[1]
    state = w_bc.shape[2] // 2
    assert w_bc.shape[1] == 1 and inner == heads * LANES
    count, parts = lax.axis_size("seq"), lax.axis_size("mp")
    sources, grads = pl.pallas_call(
        sources_kernel,
        out_shape=(shape_of(bf16, 2, length, width),) * 2,
        compiler_params=PARAMS,
    )(hidden, cotangent, ids[:, None])
    sources = sources.reshape(2 * length, width)
    grads = grads.reshape(2 * length, width)
    spare = jnp.zeros((width, LANES - heads - 2 * state), bf16)
    w_side = jnp.concatenate([w_step, spare, w_bc.reshape(width, -1)], axis=1)
    consts = jnp.pad(
        jnp.stack([step_bias, decay_log, skip]), ((0, 5), (0, LANES - heads))
    )
    aux = dot(sources, w_side).reshape(2, length, LANES)
    x = dot(sources, w_value).astype(bf16).reshape(2, length, inner)
    assert count % heads == 0 and (heads * state) % count == 0
    rows = heads * state // count
    parcel = (count, 2, 3, rows, LANES)
    states = pl.pallas_call(
        partial(ends_kernel, heads, state),
        grid=(2,),
        in_specs=[by_stream(length, LANES), shared(8, LANES), by_stream(length, inner)],
        out_specs=gathered(count, 3, rows, LANES),
        out_shape=shape_of(bf16, *parcel),
        compiler_params=PARAMS,
    )(aux, consts, x)
    starts = exchange(states, False, 0)
    dz = dot(grads, w_out, MXU_NT).astype(bf16).reshape(2, length, inner)
    z, dy, adjoint = pl.pallas_call(
        partial(outputs_kernel, heads, state),
        grid=(2,),
        in_specs=[
            by_stream(length, LANES), shared(8, LANES), by_stream(length, inner),
            by_stream(length, inner), shared(1, inner), gathered(count, 2, rows, LANES),
        ],
        out_specs=[
            by_stream(length, inner), by_stream(2, length, inner),
            gathered(count, 3, rows, LANES),
        ],
        out_shape=(
            shape_of(bf16, 2, length, inner), shape_of(bf16, 2, 2, length, inner),
            shape_of(bf16, *parcel),
        ),
        scratch_shapes=[pltpu.VMEM((2, length, inner), f32)],
        compiler_params=PARAMS,
    )(aux, consts, x, dz, norm_gain[None], starts)
    mine = lax.axis_index("mp")
    hops = range(1, parts)
    leaving = [out_share(z, w_out, lax.rem(mine + hop, parts), parts, bf16) for hop in hops]
    adjoint, leaving = lax.optimization_barrier((adjoint, leaving))
    out_received = [send_on(share, hop, parts) for hop, share in zip(hops, leaving)]
    arriving = exchange(adjoint, True, 1)
    dx, tail = pl.pallas_call(
        partial(grads_kernel, heads, state),
        grid=(2,),
        in_specs=[
            by_stream(length, LANES), shared(8, LANES), by_stream(length, inner),
            by_stream(2, length, inner), gathered(count, 2, rows, LANES),
            gathered(count, 3, rows, LANES), gathered(count, 2, rows, LANES),
        ],
        out_specs=[by_stream(length, inner), by_stream(length, LANES)],
        out_shape=(shape_of(bf16, 2, length, inner), shape_of(bf16, 2, length, LANES)),
        cost_estimate=pl.CostEstimate(
            flops=24 * length * length * inner, bytes_accessed=16 * length * inner,
            transcendentals=2 * heads * length * length,
        ),
        compiler_params=PARAMS,
    )(aux, consts, x, dy, starts, states, arriving)
    dx, tail, out_received = lax.optimization_barrier((dx, tail, out_received))
    leaving = [
        hidden_share(dx, tail, w_value, w_side, lax.rem(mine + hop, parts), parts, bf16)
        for hop in hops
    ]
    dx, tail, z, leaving = lax.optimization_barrier((dx, tail, z, leaving))
    received = [send_on(share, hop, parts) for hop, share in zip(hops, leaving)]
    out = out_share(z, w_out, mine, parts, f32)
    d_hidden = hidden_share(dx, tail, w_value, w_side, mine, parts, f32)
    for share in out_received:
        out += share.astype(f32)
    for share in received:
        d_hidden += share.astype(f32)
    return (out.astype(bf16), d_hidden.astype(bf16))


def solution(mesh):
    in_specs = (
        P("seq", None),
        P("seq"),
        P(None, "mp"),
        P(None, "mp", None),
        P(None, "mp"),
        P("mp"),
        P("mp"),
        P("mp"),
        P("mp"),
        P("mp", None),
        P("seq", None),
    )
    out_specs = (P("seq", "mp"), P("seq", "mp"))
    return jax.shard_map(
        per_device, mesh=mesh, in_specs=in_specs, out_specs=out_specs, check_vma=False
    )
```
